256 devices in a mesh: pair: 16 (over x, y), col: 16 (over z, core).
Axes of the slice: x: 4, y: 4, z: 8, core: 2. Of those that a mesh axis runs over, the one named last changes fastest.
Arguments:
- w_tiles: float32 [80, 128, 8192], P('pair', 'col'), may hold values from -0.15625 to 0.15625
- w_cols: int32 [80, 128], P('pair', 'col'), may hold values from 0 to 19, as said below
- t_tiles: float32 [320, 16, 4096], P('col', 'pair'), may hold values from -6 to 6
- t_cols: int32 [320, 16], P('col', 'pair'), may hold values from 0 to 79, as said below
- z_cols: int32 [16, 80, 5], P('pair'), may hold values from 0 to 4, as said below
Outputs:
- z_tiles: float32 [16, 80, 5, 8192], P('pair', None, None, 'col')
The draws below stay inside these ranges and needn't reach their ends.
Inputs may be any that keep to these rules, and one draw needn't show every extreme that they name: `w_cols`: the 8 entries of one row tile and one col index are distinct. `t_cols`: the 16 entries of one contraction tile are distinct. `z_cols`: the 5 entries of one group and row tile name each of the group's column tiles once.
All inputs are finite; a program needn't handle non-finite values.
Results may differ from the reference program's by a relative error of at most 0.00007.
Values sent between devices are 32-bit elements; how exact they have to be, the bound alone decides.
A program may use at most 192 MiB of HBM per device.

```python
import jax
import jax.numpy as jnp
from jax import lax

S = 64
RB = 80
CB = 80
KB_DEV = 20
NWR = 8
NTK = 16
ROWS = 128
KB = 320
CB_DEV = 5
N_PAIR = 16
N_COL = 16


def pick_distinct(key, row_count, pool_size, picked):
    scores = jax.random.randint(key, (row_count, pool_size), 0, 1 << 20) * pool_size + jnp.arange(pool_size, dtype=jnp.int32)[None, :]
    ranking = jnp.argsort(scores, axis=1).astype(jnp.int32)
    leading = ranking[0]
    shifted = (leading - leading[0] + pool_size - 1) % pool_size
    ranking = ranking.at[0].set(shifted)
    return ranking[:, :picked]


def draw_w_cols(key, part):
    return pick_distinct(jax.random.fold_in(key, 11), RB * N_COL, KB_DEV, NWR).reshape(RB, N_COL * NWR)


def draw_t_cols(key, part):
    return pick_distinct(jax.random.fold_in(key, 23), KB, CB, NTK)


def draw_z_cols(key, part):
    return pick_distinct(jax.random.fold_in(key, 37), N_PAIR * RB, CB_DEV, CB_DEV).reshape(N_PAIR, RB, CB_DEV)


def block_scale(rng, extent, shards, smallest, largest):
    def one(axis_at, blocks):
        draws = jax.random.uniform(jax.random.fold_in(jax.random.fold_in(rng, 6), axis_at), (blocks,), jnp.float32, smallest / len(shards), largest / len(shards))
        return jnp.repeat(jnp.exp(draws), extent[axis_at] // blocks).reshape((-1,) + (1,) * (len(extent) - axis_at - 1))

    level = one(*shards[0])
    for cut in shards[1:]:
        level = level * one(*cut)
    return level


def centred(own_key, shape, spread, bound, pieces=(), kind=jnp.bfloat16):
    entries = spread * jax.random.normal(own_key, shape, jnp.float32)
    if pieces:
        entries = entries * block_scale(own_key, shape, pieces, -0.22, 0.18)
    return jnp.clip(entries, -bound, bound).astype(kind)


def setup_inputs(seed: int = 0) -> dict:
    seeds = jax.random.split(jax.random.key(seed), 6)
    w_tiles = centred(seeds[0], (RB, N_COL * NWR, ROWS * S), (S * N_COL * NWR * NTK // CB) ** -0.5, 0.15625, ((0, 16), (1, 16)), jnp.float32)
    w_cols = draw_w_cols(jax.random.fold_in(seeds[5], 71), 0)
    t_tiles = centred(seeds[2], (KB, NTK, S * S), 1.0, 6.0, ((0, 16), (1, 16)), jnp.float32)
    t_cols = draw_t_cols(jax.random.fold_in(seeds[5], 71), 0)
    z_cols = draw_z_cols(jax.random.fold_in(seeds[5], 71), 0)
    return dict(w_tiles=w_tiles, w_cols=w_cols, t_tiles=t_tiles, t_cols=t_cols, z_cols=z_cols)


def reference(w_tiles, w_cols, t_tiles, t_cols, z_cols):
    slots = N_COL * NWR
    kappa = ((jnp.arange(slots, dtype=jnp.int32) // NWR) * KB_DEV)[None, :] + w_cols
    target = (jnp.arange(N_PAIR, dtype=jnp.int32) * CB_DEV)[:, None, None] + z_cols
    hits = (t_cols[:, :, None] == jnp.arange(CB, dtype=jnp.int32)[None, None, :]).astype(jnp.float32)
    dense = jnp.einsum("kjc,kje->kce", hits, t_tiles, precision=lax.Precision.HIGHEST)

    def one_row(row_index):
        tiles = dense[kappa[row_index]].reshape(slots, CB, S, S)
        w_block = w_tiles[row_index].reshape(slots, ROWS, S)
        full = jnp.einsum("sma,scab->mcb", w_block, tiles, precision=lax.Precision.HIGHEST)
        wanted = target[:, row_index, :]
        picked = full[:, wanted, :]
        picked = jnp.transpose(picked, (1, 2, 0, 3))
        return picked.reshape(N_PAIR, CB_DEV, ROWS * S)

    stacked = lax.map(one_row, jnp.arange(RB, dtype=jnp.int32))
    return jnp.transpose(stacked, (1, 0, 2, 3))
```

```python
import functools

import jax
import jax.numpy as jnp
from jax import lax
from jax.experimental import pallas as pl
from jax.experimental.pallas import tpu as pltpu
from jax.sharding import PartitionSpec as P

MESH = pl.DeviceIdType.MESH

S = 64
LANES = 128
SIDE = 4
PAIRS = 16
NZ = 8
RT = 5
KC = 20
WS = 8
CW = 5
NB = 8
PL = 5
ROWS = 640
HALF = ROWS // 2
CH = 40
KDIM = KC * S
SHARD = KC * 32
COLS = 80
HS = SHARD // 2
QS = HS // 2
STEPS_A = 4
STEPS_B = 3
DEPTH = 4
PARTS = ((0, 2), (2, 4), (4, 5))
F32 = jnp.float32
BF16 = jnp.bfloat16
PLACES = ((0, 1), (2, 3), (4, 9), (5, 6), (7, 8))


def mix(a, b, left):
    straight = jnp.where(left, a, b)
    crossed = pltpu.roll(jnp.where(left, b, a), S, 1)
    return jnp.where(left, straight, crossed), jnp.where(left, crossed, straight)


def split(x):
    high = x.astype(BF16)
    return high, (x - high.astype(F32)).astype(BF16)


def main_kernel(
    t_ref,
    ids_ref,
    w_ref,
    w_cols_ref,
    out_ref,
    shard,
    tiles,
    ids_own,
    ids,
    inv_vec,
    inv,
    w_rows,
    w_wide,
    w_pair,
    halves,
    t_high,
    t_low,
    part,
    swap,
    acc_a,
    acc_b,
    total,
    g_send,
    g_recv,
    own_sem,
    inv_sem,
    i_send,
    i_recv,
    s_send,
    s_recv,
    a_send,
    a_recv,
    b_send,
    b_recv,
    x_send,
    x_recv,
    home_sem,
):
    p = lax.axis_index("pair")
    q = lax.axis_index("col")
    px, py = p // SIDE, lax.rem(p, SIDE)
    z, core = q // 2, lax.rem(q, 2)
    left = lax.broadcasted_iota(jnp.int32, (1, LANES), 1) < S

    def near(axis, sign):
        if axis == 0:
            there = lax.rem(px + sign + SIDE, SIDE) * SIDE + py
        else:
            there = px * SIDE + lax.rem(py + sign + SIDE, SIDE)
        return {"pair": there, "col": q}

    def along_z(step):
        return {"pair": p, "col": lax.rem(z + step + 2 * NZ, NZ) * 2 + core}

    mate = {"pair": p, "col": z * 2 + 1 - core}

    barrier = pltpu.get_barrier_semaphore()
    for d in range(1, PAIRS):
        pl.semaphore_signal(
            barrier, inc=1, device_id={"pair": lax.rem(p + d, PAIRS), "col": q}, device_id_type=MESH
        )
    for who in (mate, along_z(1), along_z(-1)):
        pl.semaphore_signal(barrier, inc=1, device_id=who, device_id_type=MESH)

    ids_own[...] = jnp.zeros_like(ids_own)
    ids_own[0:1, 0:KC] = ids_ref[...]

    for k in range(KC):
        top = t_ref[k * 32 : k * 32 + 16]
        bottom = t_ref[k * 32 + 16 : k * 32 + 32]
        for h, rows in enumerate(mix(top, bottom, left)):
            shard[pl.ds(k * 32 + h, 16, stride=2), :] = rows

    pl.semaphore_wait(barrier, PAIRS + 2)
    own_copy = pltpu.make_async_copy(shard, tiles.at[p], own_sem)
    own_copy.start()

    def slot(half, da, db):
        dx, dy = (da, db) if half == 0 else (db, da)
        return lax.rem(px + dx + SIDE, SIDE) * SIDE + lax.rem(py + dy + SIDE, SIDE)

    def hop(number, half, da, db, first, count, axis, sign):
        place = slot(half, da, db)
        rows = pl.ds(first, count)
        source = shard.at[rows] if (da, db) == (0, 0) else tiles.at[place, rows]
        return pltpu.make_async_remote_copy(
            src_ref=source,
            dst_ref=tiles.at[place, rows],
            send_sem=g_send.at[number],
            recv_sem=g_recv.at[number],
            device_id=near(axis, sign),
            device_id_type=MESH,
        )

    def landing(number, half, da, db, first, count, axis, sign):
        return pltpu.make_async_remote_copy(
            src_ref=tiles.at[slot(half, da, db), pl.ds(first, count)],
            dst_ref=tiles.at[slot(half, da, db), pl.ds(first, count)],
            send_sem=g_send.at[number],
            recv_sem=g_recv.at[number],
            device_id=near(axis, sign),
            device_id_type=MESH,
        )

    sends = []
    numbers = {}

    def go(half, kind, da, sign):
        axis_a, axis_b = (0, 1) if half == 0 else (1, 0)
        base = half * HS
        quarter = base if sign == 1 else base + QS
        if kind == "a0":
            args = (0, 0, base, HS, axis_a)
            seen = (-sign, 0)
        elif kind == "a1":
            args = (-sign, 0, quarter, QS, axis_a)
            seen = (2, 0)
        elif kind == "b0":
            args = (da, 0, base, HS, axis_b)
            seen = (da, -sign)
        else:
            args = (da, -sign, quarter, QS, axis_b)
            seen = (da, 2)
        number = len(numbers)
        numbers[half, kind, da, sign] = (number, half, *seen, *args[2:], sign)
        copy = hop(number, half, *args, sign)
        copy.start()
        sends.append(copy)

    def got(half, kind, da, sign):
        landing(*numbers[half, kind, da, sign]).wait_recv()

    both = (1, -1)
    for sign in both:
        for half in range(2):
            go(half, "a0", 0, sign)
            go(half, "b0", 0, sign)

    def send_ids(d):
        there = lax.rem(p + d, PAIRS)
        return pltpu.make_async_remote_copy(
            src_ref=ids_own,
            dst_ref=ids.at[p],
            send_sem=i_send.at[there],
            recv_sem=i_recv.at[p],
            device_id={"pair": there, "col": q},
            device_id_type=MESH,
        )

    def get_ids(d):
        source = lax.rem(p + d, PAIRS)
        return pltpu.make_async_remote_copy(
            src_ref=ids_own,
            dst_ref=ids.at[source],
            send_sem=i_send.at[source],
            recv_sem=i_recv.at[source],
            device_id={"pair": source, "col": q},
            device_id_type=MESH,
        )

    for d in range(1, PAIRS):
        send_ids(d).start()
    ids[p] = ids_own[...]

    @pl.loop(0, 64)
    def _(m):
        lanes = pl.ds(pl.multiple_of(m * LANES, LANES), LANES)
        for r in range(RT):
            w_rows[r, pl.ds(m, WS, stride=64), :] = w_ref[r, :, lanes]

    def w_dense(w):
        for r in range(RT):
            picks = [jnp.zeros((64, LANES), F32)] * 2
            for n in range(WS):
                rows = w_rows[r, n * 64 : (n + 1) * 64, :]
                for k in range(2):
                    there = jnp.where(w_cols_ref[r, n] == 2 * w + k, 1.0, 0.0)
                    picks[k] = picks[k] + there * rows
            for odd, rows in enumerate(mix(*picks, left)):
                for zz in range(NZ):
                    for c in range(2):
                        to = c * HALF + zz * CH + r * 8 + odd * 4
                        w_wide[w, to : to + 4, :] = rows[zz * 8 + c * 4 : zz * 8 + c * 4 + 4]

    def w_split(w):
        high, low = split(w_wide[w])
        w_pair[0:ROWS, w * LANES : (w + 1) * LANES] = high
        w_pair[ROWS : 2 * ROWS, w * LANES : (w + 1) * LANES] = low

    def halve(half, da, db):
        place = slot(half, da, db)

        @pl.loop(half * KC // 2, (half + 1) * KC // 2)
        def _(k):
            rows = pl.ds(pl.multiple_of(k * 32, 32), 32)
            x = tiles[place, rows, :]
            turned = pltpu.roll(x, S, 1)
            for h, wide in enumerate((jnp.where(left, x, turned), jnp.where(left, turned, x))):
                high, low = split(wide)
                halves[place, 2 * h, rows, :] = high
                halves[place, 2 * h + 1, rows, :] = low

    for sign in both:
        for half in range(2):
            got(half, "a0", 0, sign)
            go(half, "a1", 0, sign)
            go(half, "b0", -sign, 1)
            go(half, "b0", -sign, -1)

    @pl.loop(0, KC // 4)
    def _(w):
        w_dense(w)

    for sign in both:
        for half in range(2):
            got(half, "b0", 0, sign)
            go(half, "b1", 0, sign)
    for half in range(2):
        for sign in both:
            got(half, "a1", 0, sign)
        for sign in both:
            go(half, "b0", 2, sign)

    @pl.loop(KC // 4, KC // 2)
    def _(w):
        w_dense(w)

    halves[PAIRS] = jnp.zeros((4, SHARD, LANES), BF16)
    own_copy.wait()
    for half in range(2):
        halve(half, 0, 0)
        halve(half, -1, 0)
        halve(half, 1, 0)
        halve(half, 0, -1)
        halve(half, 0, 1)
    for da in (-1, 1):
        for sign in both:
            for half in range(2):
                got(half, "b0", da, sign)
                go(half, "b1", da, sign)
    for w in range(KC // 2):
        w_split(w)
    for sign in both:
        for half in range(2):
            got(half, "b0", 2, sign)
            go(half, "b1", 2, sign)

    for d in range(1, PAIRS):
        get_ids(d).wait_recv()
    tile_at = lax.broadcasted_iota(jnp.int32, (COLS, LANES), 0)
    found = jnp.full((COLS, LANES), PAIRS, jnp.int32)
    for n in range(PAIRS):
        found = jnp.where(ids[n, 0:1, :] == tile_at, n, found)
    inv_vec[...] = found
    table = pltpu.make_async_copy(inv_vec, inv, inv_sem)
    table.start()
    table.wait()
    for half in range(2):
        halve(half, 2, 0)
        for da in (-1, 1, 2):
            halve(half, da, -1)
            halve(half, da, 1)
    for da in (0, -1, 1, 2):
        for half in range(2):
            for sign in both:
                got(half, "b1", da, sign)
            halve(half, da, 2)

    def pair_swap(b, n):
        planes = pl.ds(PARTS[n][0], PARTS[n][1] - PARTS[n][0])
        return pltpu.make_async_remote_copy(
            src_ref=part.at[b, planes, pl.ds((1 - core) * HALF, HALF)],
            dst_ref=swap.at[b, planes],
            send_sem=s_send.at[b, n],
            recv_sem=s_recv.at[b, n],
            device_id=mate,
            device_id_type=MESH,
        )

    def way(b):
        return 1 - 2 * lax.rem(b, 2)

    def own_rows(step):
        return pl.ds(core * HALF + lax.rem(z + step + 2 * NZ, NZ) * CH, CH)

    def chain(b, k, length, acc, send, recv, sign):
        source = part.at[b, :, own_rows(length * sign)] if k == 0 else acc.at[b, k - 1]
        return pltpu.make_async_remote_copy(
            src_ref=source,
            dst_ref=acc.at[b, k],
            send_sem=send.at[b, k],
            recv_sem=recv.at[b, k],
            device_id=along_z(sign),
            device_id_type=MESH,
        )

    def chain_a(b, k):
        return chain(b, k, STEPS_A, acc_a, a_send, a_recv, way(b))

    def chain_b(b, k):
        return chain(b, k, STEPS_B, acc_b, b_send, b_recv, -way(b))

    def group_pair(b):
        return lax.rem(b + p // 2, NB)

    def outward(b, odd):
        there = group_pair(b) * 2 + odd
        return there, pltpu.make_async_remote_copy(
            src_ref=total.at[b, pl.ds(2 * odd, 3)],
            dst_ref=out_ref.at[:, pl.ds(p * CH, CH)],
            send_sem=x_send.at[b, odd],
            recv_sem=x_recv.at[p],
            device_id={"pair": there, "col": q},
            device_id_type=MESH,
        )

    def homeward(b, odd):
        return pltpu.make_async_copy(
            total.at[b, pl.ds(2 * odd, 3)], out_ref.at[:, pl.ds(p * CH, CH)], home_sem
        )

    def only(b, act):
        @pl.when(jnp.logical_and(b >= 0, b < NB))
        def _():
            act(b)

    def begin(b):
        for n in range(len(PARTS)):
            pair_swap(b, n).wait_recv()
        part[b, :, pl.ds(core * HALF, HALF), :] += swap[b]
        chain_a(b, 0).start()
        chain_b(b, 0).start()

    def onward(k):
        def act(b):
            sign = way(b)
            chain_a(b, k).wait_recv()
            acc_a[b, k] += part[b, :, own_rows((STEPS_A - 1 - k) * sign), :]
            chain_a(b, k + 1).start()
            chain_b(b, k).wait_recv()
            if k < STEPS_B - 1:
                acc_b[b, k] += part[b, :, own_rows(-(STEPS_B - 1 - k) * sign), :]
                chain_b(b, k + 1).start()

        return act

    def finish(b):
        chain_a(b, 3).wait_recv()
        total[b] = part[b, :, own_rows(0), :] + acc_a[b, 3] + acc_b[b, 2]
        for odd in range(2):
            there, copy = outward(b, odd)

            @pl.when(there != p)
            def _():
                copy.start()

            @pl.when(there == p)
            def _():
                homeward(b, odd).start()

    def expand(b):
        base = group_pair(b) * 2 * CW

        @pl.loop(0, KC)
        def _(k):
            rows = pl.ds(pl.multiple_of(k * 32, 32), 32)
            for i, (one, two) in enumerate(PLACES):
                a = inv[base + one, k]
                c = inv[base + two, k]
                for h in range(2):
                    to = pl.ds(pl.multiple_of(k * S + h * 32, 32), 32)
                    for n, wide in enumerate((t_high, t_low)):
                        wide[to, i * LANES : (i + 1) * LANES] = jnp.where(
                            left, halves[a, 2 * h + n, rows, :], halves[c, 2 * h + n, rows, :]
                        )

    def multiply(n):
        def act(b):
            first, last = PARTS[n]
            cols = slice(first * LANES, last * LANES)
            wide = jnp.dot(w_pair[...], t_high[:, cols], preferred_element_type=F32)
            thin = jnp.dot(w_pair[0:ROWS, :], t_low[:, cols], preferred_element_type=F32)
            sums = wide[0:ROWS] + (wide[ROWS:] + thin)
            for i in range(first, last):
                part[b, i] = sums[:, (i - first) * LANES : (i - first + 1) * LANES]
            pair_swap(b, n).start()

        return act

    @pl.loop(0, NB + DEPTH)
    def _(t):
        only(t - 4, finish)
        only(t - 2, onward(0))
        only(t, expand)
        only(t - 1, begin)
        only(t, multiply(0))
        only(t - 3, onward(2))
        only(t, multiply(1))
        only(t - 2, onward(1))
        only(t, multiply(2))

    for d in range(1, PAIRS):
        source = lax.rem(p + d, PAIRS)
        pltpu.make_async_remote_copy(
            src_ref=total.at[0, pl.ds(0, 3)],
            dst_ref=out_ref.at[:, pl.ds(source * CH, CH)],
            send_sem=x_send.at[0, 0],
            recv_sem=x_recv.at[source],
            device_id={"pair": source, "col": q},
            device_id_type=MESH,
        ).wait_recv()

    @pl.loop(0, NB)
    def _(b):
        for n in range(len(PARTS)):
            pair_swap(b, n).wait_send()
        for k in range(STEPS_A):
            chain_a(b, k).wait_send()
        for k in range(STEPS_B):
            chain_b(b, k).wait_send()
        for odd in range(2):
            there, copy = outward(b, odd)

            @pl.when(there != p)
            def _():
                copy.wait_send()

            @pl.when(there == p)
            def _():
                homeward(b, odd).wait()

    for copy in sends:
        copy.wait_send()
    for d in range(1, PAIRS):
        send_ids(d).wait_send()


def pick_kernel(rows_ref, z_cols_ref, out_ref):
    odd = lax.rem(lax.axis_index("pair"), 2)
    left = lax.broadcasted_iota(jnp.int32, (1, LANES), 1) < S
    planes = (
        jnp.where(odd == 1, 1, 0),
        jnp.where(odd == 1, 2, 1),
        jnp.where(odd == 1, 0, 2),
    )
    count = out_ref.shape[1]
    across = lax.broadcasted_iota(jnp.int32, (count, count), 1)
    diagonal = lax.broadcasted_iota(jnp.int32, (count, count), 0) == across
    wants = []
    for zz in range(CW):
        row = z_cols_ref[zz : zz + 1, :].astype(F32)
        want = jnp.sum(jnp.where(diagonal, row, 0.0), axis=1, keepdims=True)
        wants.append(jnp.broadcast_to(want, (count, LANES)))
    for j in range(4):
        found = []
        for n, plane in enumerate(planes):
            one = rows_ref[plane, pl.ds(j, count, stride=8), :]
            two = rows_ref[plane, pl.ds(4 + j, count, stride=8), :]
            lefts, rights = mix(one, two, left)
            if n < 2:
                found += [lefts, rights]
            else:
                found.append(jnp.where(odd == 1, rights, lefts))
        for zz in range(CW):
            value = found[0]
            for c in range(1, CW):
                value = jnp.where(wants[zz] == c, found[c], value)
            out_ref[zz, :, j * LANES : (j + 1) * LANES] = value


def on_device(w_tiles, w_cols, t_tiles, t_cols, z_cols):
    t = t_tiles.reshape(SHARD, LANES)
    ids = t_cols.reshape(1, KC)
    vmem = pl.BlockSpec(memory_space=pltpu.VMEM)
    dma = pltpu.SemaphoreType.DMA
    rows = pl.pallas_call(
        main_kernel,
        out_shape=jax.ShapeDtypeStruct((3, PAIRS * CH, LANES), F32),
        in_specs=[vmem, vmem, vmem, pl.BlockSpec(memory_space=pltpu.SMEM)],
        out_specs=pl.BlockSpec(memory_space=pl.ANY),
        scratch_shapes=[
            pltpu.VMEM((SHARD, LANES), F32),
            pltpu.VMEM((PAIRS, SHARD, LANES), F32),
            pltpu.VMEM((8, LANES), jnp.int32),
            pltpu.VMEM((PAIRS, 8, LANES), jnp.int32),
            pltpu.VMEM((COLS, LANES), jnp.int32),
            pltpu.SMEM((COLS, LANES), jnp.int32),
            pltpu.VMEM((RT, WS * 64, LANES), F32),
            pltpu.VMEM((KC // 2, ROWS, LANES), F32),
            pltpu.VMEM((2 * ROWS, KDIM), BF16),
            pltpu.VMEM((PAIRS + 1, 4, SHARD, LANES), BF16),
            pltpu.VMEM((KDIM, PL * LANES), BF16),
            pltpu.VMEM((KDIM, PL * LANES), BF16),
            pltpu.VMEM((NB, PL, ROWS, LANES), F32),
            pltpu.VMEM((NB, PL, HALF, LANES), F32),
            pltpu.VMEM((NB, STEPS_A, PL, CH, LANES), F32),
            pltpu.VMEM((NB, STEPS_B, PL, CH, LANES), F32),
            pltpu.VMEM((NB, PL, CH, LANES), F32),
            dma((40,)),
            dma((40,)),
            dma,
            dma,
            dma((PAIRS,)),
            dma((PAIRS,)),
            dma((NB, len(PARTS))),
            dma((NB, len(PARTS))),
            dma((NB, STEPS_A)),
            dma((NB, STEPS_A)),
            dma((NB, STEPS_B)),
            dma((NB, STEPS_B)),
            dma((NB, 2)),
            dma((PAIRS,)),
            dma,
        ],
        compiler_params=pltpu.CompilerParams(
            collective_id=0, has_side_effects=True, vmem_limit_bytes=66 * 1000 * 1000
        ),
        name="cycle",
    )(t, ids, w_tiles, w_cols)
    picked = pl.pallas_call(
        pick_kernel,
        out_shape=jax.ShapeDtypeStruct((CW, PAIRS * RT, 8 * S), F32),
        in_specs=[vmem, vmem],
        out_specs=vmem,
        name="pick",
    )(rows, z_cols[0].T)
    return picked.transpose(1, 0, 2)[None]


def solution(mesh):
    in_specs = (
        P("pair", "col", None),
        P("pair", "col"),
        P("col", "pair", None),
        P("col", "pair"),
        P("pair", None, None),
    )
    out_specs = P("pair", None, None, "col")
    return jax.shard_map(
        on_device, mesh=mesh, in_specs=in_specs, out_specs=out_specs, check_vma=False
    )
```

```python
import functools

import jax
import jax.numpy as jnp
from jax import lax
from jax.experimental import pallas as pl
from jax.experimental.pallas import tpu as pltpu
from jax.sharding import PartitionSpec as P

MESH = pl.DeviceIdType.MESH

S = 64
LANES = 128
SIDE = 4
PAIRS = 16
NZ = 8
RT = 5
KC = 20
WS = 8
CW = 5
NB = 8
PL = 5
ROWS = 640
HALF = ROWS // 2
CH = 40
KDIM = KC * S
SHARD = KC * 32
COLS = 80
HS = SHARD // 2
QS = HS // 2
STEPS_A = 4
STEPS_B = 3
DEPTH = 5
PARTS = ((0, 3), (3, 5))
LATE = (9, 7, 5, 3)
DOTS = (((0, 2), (2, 3)), ((3, 5),))
F32 = jnp.float32
BF16 = jnp.bfloat16
PLACES = ((0, 1), (2, 3), (4, 9), (5, 6), (7, 8))


def mix(a, b, left):
    straight = jnp.where(left, a, b)
    crossed = pltpu.roll(jnp.where(left, b, a), S, 1)
    return jnp.where(left, straight, crossed), jnp.where(left, crossed, straight)


def split(x):
    high = x.astype(BF16)
    return high, (x - high.astype(F32)).astype(BF16)


def main_kernel(
    t_ref,
    ids_ref,
    w_ref,
    w_cols_ref,
    out_ref,
    shard,
    tiles,
    ids_own,
    ids,
    inv_vec,
    inv,
    w_rows,
    w_wide,
    w_pair,
    halves,
    t_high,
    t_low,
    part,
    swap,
    acc_a,
    acc_b,
    total,
    g_send,
    g_recv,
    own_sem,
    inv_sem,
    i_send,
    i_recv,
    s_send,
    s_recv,
    a_send,
    a_recv,
    b_send,
    b_recv,
    x_send,
    x_recv,
    home_sem,
):
    p = lax.axis_index("pair")
    q = lax.axis_index("col")
    px, py = p // SIDE, lax.rem(p, SIDE)
    z, core = q // 2, lax.rem(q, 2)
    left = lax.broadcasted_iota(jnp.int32, (1, LANES), 1) < S

    def near(axis, sign):
        if axis == 0:
            there = lax.rem(px + sign + SIDE, SIDE) * SIDE + py
        else:
            there = px * SIDE + lax.rem(py + sign + SIDE, SIDE)
        return {"pair": there, "col": q}

    def along_z(step):
        return {"pair": p, "col": lax.rem(z + step + 2 * NZ, NZ) * 2 + core}

    mate = {"pair": p, "col": z * 2 + 1 - core}

    barrier = pltpu.get_barrier_semaphore()
    for d in range(1, PAIRS):
        pl.semaphore_signal(
            barrier, inc=1, device_id={"pair": lax.rem(p + d, PAIRS), "col": q}, device_id_type=MESH
        )
    for who in (mate, along_z(1), along_z(-1)):
        pl.semaphore_signal(barrier, inc=1, device_id=who, device_id_type=MESH)

    ids_own[...] = jnp.zeros_like(ids_own)
    ids_own[0:1, 0:KC] = ids_ref[...]

    for k in range(KC):
        top = t_ref[k * 32 : k * 32 + 16]
        bottom = t_ref[k * 32 + 16 : k * 32 + 32]
        for h, rows in enumerate(mix(top, bottom, left)):
            shard[pl.ds(k * 32 + h, 16, stride=2), :] = rows

    pl.semaphore_wait(barrier, PAIRS + 2)
    own_copy = pltpu.make_async_copy(shard, tiles.at[p], own_sem)
    own_copy.start()

    def slot(half, da, db):
        dx, dy = (da, db) if half == 0 else (db, da)
        return lax.rem(px + dx + SIDE, SIDE) * SIDE + lax.rem(py + dy + SIDE, SIDE)

    def hop(number, half, da, db, first, count, axis, sign):
        place = slot(half, da, db)
        rows = pl.ds(first, count)
        source = shard.at[rows] if (da, db) == (0, 0) else tiles.at[place, rows]
        return pltpu.make_async_remote_copy(
            src_ref=source,
            dst_ref=tiles.at[place, rows],
            send_sem=g_send.at[number],
            recv_sem=g_recv.at[number],
            device_id=near(axis, sign),
            device_id_type=MESH,
        )

    def landing(number, half, da, db, first, count, axis, sign):
        return pltpu.make_async_remote_copy(
            src_ref=tiles.at[slot(half, da, db), pl.ds(first, count)],
            dst_ref=tiles.at[slot(half, da, db), pl.ds(first, count)],
            send_sem=g_send.at[number],
            recv_sem=g_recv.at[number],
            device_id=near(axis, sign),
            device_id_type=MESH,
        )

    sends = []
    numbers = {}

    def go(half, kind, da, sign):
        axis_a, axis_b = (0, 1) if half == 0 else (1, 0)
        base = half * HS
        quarter = base if sign == 1 else base + QS
        if kind == "a0":
            args = (0, 0, base, HS, axis_a)
            seen = (-sign, 0)
        elif kind == "a1":
            args = (-sign, 0, quarter, QS, axis_a)
            seen = (2, 0)
        elif kind == "b0":
            args = (da, 0, base, HS, axis_b)
            seen = (da, -sign)
        else:
            args = (da, -sign, quarter, QS, axis_b)
            seen = (da, 2)
        number = len(numbers)
        numbers[half, kind, da, sign] = (number, half, *seen, *args[2:], sign)
        copy = hop(number, half, *args, sign)
        copy.start()
        sends.append(copy)

    def got(half, kind, da, sign):
        landing(*numbers[half, kind, da, sign]).wait_recv()

    both = (1, -1)
    for sign in both:
        for half in range(2):
            go(half, "a0", 0, sign)
            go(half, "b0", 0, sign)

    def send_ids(d):
        there = lax.rem(p + d, PAIRS)
        return pltpu.make_async_remote_copy(
            src_ref=ids_own,
            dst_ref=ids.at[p],
            send_sem=i_send.at[there],
            recv_sem=i_recv.at[p],
            device_id={"pair": there, "col": q},
            device_id_type=MESH,
        )

    def get_ids(d):
        source = lax.rem(p + d, PAIRS)
        return pltpu.make_async_remote_copy(
            src_ref=ids_own,
            dst_ref=ids.at[source],
            send_sem=i_send.at[source],
            recv_sem=i_recv.at[source],
            device_id={"pair": source, "col": q},
            device_id_type=MESH,
        )

    for d in range(1, PAIRS):
        send_ids(d).start()
    ids[p] = ids_own[...]

    @pl.loop(0, 64)
    def _(m):
        lanes = pl.ds(pl.multiple_of(m * LANES, LANES), LANES)
        for r in range(RT):
            w_rows[r, pl.ds(m, WS, stride=64), :] = w_ref[r, :, lanes]

    def w_dense(w):
        for r in range(RT):
            picks = [jnp.zeros((64, LANES), F32)] * 2
            for n in range(WS):
                rows = w_rows[r, n * 64 : (n + 1) * 64, :]
                for k in range(2):
                    there = jnp.where(w_cols_ref[r, n] == 2 * w + k, 1.0, 0.0)
                    picks[k] = picks[k] + there * rows
            for odd, rows in enumerate(mix(*picks, left)):
                for zz in range(NZ):
                    for c in range(2):
                        to = c * HALF + zz * CH + r * 8 + odd * 4
                        w_wide[w, to : to + 4, :] = rows[zz * 8 + c * 4 : zz * 8 + c * 4 + 4]

    def w_split(w):
        high, low = split(w_wide[w])
        w_pair[0:ROWS, w * LANES : (w + 1) * LANES] = high
        w_pair[ROWS : 2 * ROWS, w * LANES : (w + 1) * LANES] = low

    def halve(half, da, db):
        place = slot(half, da, db)

        @pl.loop(half * 4, half * 4 + 4)
        def _(n):
            rows = pl.ds(pl.multiple_of(n * 80, 80), 80)
            x = tiles[place, rows, :]
            for h, wide in enumerate((x, pltpu.roll(x, S, 1))):
                high, low = split(wide)
                halves[place, 2 * h, rows, :] = high
                halves[place, 2 * h + 1, rows, :] = low

    for sign in both:
        for half in range(2):
            got(half, "a0", 0, sign)
            go(half, "a1", 0, sign)
            go(half, "b0", -sign, 1)
            go(half, "b0", -sign, -1)
    own_copy.wait()
    for half in range(2):
        halve(half, 0, 0)
        halve(half, -1, 0)
        halve(half, 1, 0)

    @pl.loop(0, KC // 4)
    def _(w):
        w_dense(w)

    for sign in both:
        for half in range(2):
            got(half, "b0", 0, sign)
            go(half, "b1", 0, sign)
    for half in range(2):
        for sign in both:
            got(half, "a1", 0, sign)
        for sign in both:
            go(half, "b0", 2, sign)
    for half in range(2):
        halve(half, 0, -1)
        halve(half, 0, 1)
        halve(half, 2, 0)

    @pl.loop(KC // 4, KC // 2)
    def _(w):
        w_dense(w)

    for da in (-1, 1):
        for sign in both:
            for half in range(2):
                got(half, "b0", da, sign)
                go(half, "b1", da, sign)
        for sign in both:
            for half in range(2):
                halve(half, da, -sign)
    halves[PAIRS] = jnp.zeros((4, SHARD, LANES), BF16)
    for w in range(KC // 2):
        w_split(w)
    for sign in both:
        for half in range(2):
            got(half, "b0", 2, sign)
            go(half, "b1", 2, sign)

    for d in range(1, PAIRS):
        get_ids(d).wait_recv()
    tile_at = lax.broadcasted_iota(jnp.int32, (COLS, LANES), 0)
    found = jnp.full((COLS, LANES), PAIRS, jnp.int32)
    for n in range(PAIRS):
        found = jnp.where(ids[n, 0:1, :] == tile_at, n, found)
    inv_vec[...] = found
    table = pltpu.make_async_copy(inv_vec, inv, inv_sem)
    table.start()
    table.wait()
    for sign in both:
        for half in range(2):
            halve(half, 2, -sign)
    for da in (0, -1, 1, 2):
        for half in range(2):
            for sign in both:
                got(half, "b1", da, sign)
            halve(half, da, 2)

    def planes_of(h):
        return pl.ds(PARTS[h][0], PARTS[h][1] - PARTS[h][0])

    def pair_swap(b, h):
        return pltpu.make_async_remote_copy(
            src_ref=part.at[b, planes_of(h), pl.ds((1 - core) * HALF, HALF)],
            dst_ref=swap.at[b, planes_of(h)],
            send_sem=s_send.at[b, h],
            recv_sem=s_recv.at[b, h],
            device_id=mate,
            device_id_type=MESH,
        )

    def way(b, h):
        return 1 - 2 * lax.rem(b + h, 2)

    def own_rows(step):
        return pl.ds(core * HALF + lax.rem(z + step + 2 * NZ, NZ) * CH, CH)

    def chain(b, h, k, length, acc, send, recv, sign):
        planes = planes_of(h)
        source = part.at[b, planes, own_rows(length * sign)] if k == 0 else acc.at[b, k - 1, planes]
        return pltpu.make_async_remote_copy(
            src_ref=source,
            dst_ref=acc.at[b, k, planes],
            send_sem=send.at[b, h, k],
            recv_sem=recv.at[b, h, k],
            device_id=along_z(sign),
            device_id_type=MESH,
        )

    def chain_a(b, h, k):
        return chain(b, h, k, STEPS_A, acc_a, a_send, a_recv, way(b, h))

    def chain_b(b, h, k):
        return chain(b, h, k, STEPS_B, acc_b, b_send, b_recv, -way(b, h))

    def group_pair(b):
        return lax.rem(b + p // 2, NB)

    def outward(b, odd):
        there = group_pair(b) * 2 + odd
        return there, pltpu.make_async_remote_copy(
            src_ref=total.at[b, pl.ds(2 * odd, 3)],
            dst_ref=out_ref.at[:, pl.ds(p * CH, CH)],
            send_sem=x_send.at[b, odd],
            recv_sem=x_recv.at[p],
            device_id={"pair": there, "col": q},
            device_id_type=MESH,
        )

    def homeward(b, odd):
        return pltpu.make_async_copy(
            total.at[b, pl.ds(2 * odd, 3)], out_ref.at[:, pl.ds(p * CH, CH)], home_sem
        )

    def begin(b, h):
        pair_swap(b, h).wait_recv()
        part[b, planes_of(h), pl.ds(core * HALF, HALF), :] += swap[b, planes_of(h)]
        chain_a(b, h, 0).start()
        chain_b(b, h, 0).start()

    def onward(k):
        def act(b, h):
            sign = way(b, h)
            planes = planes_of(h)
            chain_a(b, h, k).wait_recv()
            acc_a[b, k, planes] += part[b, planes, own_rows((STEPS_A - 1 - k) * sign), :]
            chain_a(b, h, k + 1).start()
            chain_b(b, h, k).wait_recv()
            if k < STEPS_B - 1:
                acc_b[b, k, planes] += part[b, planes, own_rows(-(STEPS_B - 1 - k) * sign), :]
                chain_b(b, h, k + 1).start()

        return act

    def finish(b, h):
        planes = planes_of(h)
        chain_a(b, h, 3).wait_recv()
        total[b, planes] = part[b, planes, own_rows(0), :] + acc_a[b, 3, planes] + acc_b[b, 2, planes]
        there, copy = outward(b, h)

        @pl.when(there != p)
        def _():
            copy.start()

        @pl.when(there == p)
        def _():
            homeward(b, h).start()

    def expand(b, h):
        base = group_pair(b) * 2 * CW

        @pl.loop(0, KC)
        def _(k):
            rows = pl.ds(pl.multiple_of(k * 32, 32), 32)
            for i in range(*PARTS[h]):
                one, two = PLACES[i]
                a = inv[base + one, k]
                c = inv[base + two, k]
                for g in range(2):
                    to = pl.ds(pl.multiple_of(k * S + g * 32, 32), 32)
                    for n, wide in enumerate((t_high, t_low)):
                        wide[to, i * LANES : (i + 1) * LANES] = jnp.where(
                            left,
                            halves[a, 2 * g + n, rows, :],
                            halves[c, 2 - 2 * g + n, rows, :],
                        )

    def multiply(n):
        def act(b, h):
            first, last = DOTS[h][n]
            cols = slice(first * LANES, last * LANES)
            wide = jnp.dot(w_pair[...], t_high[:, cols], preferred_element_type=F32)
            thin = jnp.dot(w_pair[0:ROWS, :], t_low[:, cols], preferred_element_type=F32)
            sums = wide[0:ROWS] + (wide[ROWS:] + thin)
            for i in range(first, last):
                part[b, i] = sums[:, (i - first) * LANES : (i - first + 1) * LANES]
            if n == len(DOTS[h]) - 1:
                pair_swap(b, h).start()

        return act

    @pl.loop(0, NB + DEPTH)
    def _(t):
        for h in range(2):

            def only(late, act):
                b, part_of = t + (h - late) // 2, (h - late) % 2

                @pl.when(jnp.logical_and(b >= 0, b < NB))
                def _():
                    act(b, part_of)

            only(LATE[0], finish)
            only(LATE[1], onward(2))
            only(LATE[2], onward(1))
            only(LATE[3], onward(0))
            only(0, expand)
            only(0, multiply(0))
            only(1, begin)
            if len(DOTS[h]) > 1:
                only(0, multiply(1))

    for d in range(1, PAIRS):
        source = lax.rem(p + d, PAIRS)
        pltpu.make_async_remote_copy(
            src_ref=total.at[0, pl.ds(0, 3)],
            dst_ref=out_ref.at[:, pl.ds(source * CH, CH)],
            send_sem=x_send.at[0, 0],
            recv_sem=x_recv.at[source],
            device_id={"pair": source, "col": q},
            device_id_type=MESH,
        ).wait_recv()

    @pl.loop(0, NB)
    def _(b):
        for h in range(2):
            pair_swap(b, h).wait_send()
            for k in range(STEPS_A):
                chain_a(b, h, k).wait_send()
            for k in range(STEPS_B):
                chain_b(b, h, k).wait_send()
            there, copy = outward(b, h)

            @pl.when(there != p)
            def _():
                copy.wait_send()

            @pl.when(there == p)
            def _():
                homeward(b, h).wait()

    for copy in sends:
        copy.wait_send()
    for d in range(1, PAIRS):
        send_ids(d).wait_send()


def pick_kernel(rows_ref, z_cols_ref, out_ref):
    odd = lax.rem(lax.axis_index("pair"), 2)
    left = lax.broadcasted_iota(jnp.int32, (1, LANES), 1) < S
    planes = (
        jnp.where(odd == 1, 1, 0),
        jnp.where(odd == 1, 2, 1),
        jnp.where(odd == 1, 0, 2),
    )
    count = out_ref.shape[1]
    across = lax.broadcasted_iota(jnp.int32, (count, count), 1)
    diagonal = lax.broadcasted_iota(jnp.int32, (count, count), 0) == across
    wants = []
    for zz in range(CW):
        row = z_cols_ref[zz].astype(F32)
        want = jnp.sum(jnp.where(diagonal, row, 0.0), axis=1, keepdims=True)
        wants.append(jnp.broadcast_to(want, (count, LANES)))
    for j in range(4):
        found = []
        for n, plane in enumerate(planes):
            one = rows_ref[plane, pl.ds(j, count, stride=8), :]
            two = rows_ref[plane, pl.ds(4 + j, count, stride=8), :]
            lefts, rights = mix(one, two, left)
            if n < 2:
                found += [lefts, rights]
            else:
                found.append(jnp.where(odd == 1, rights, lefts))
        for zz in range(CW):
            value = found[0]
            for c in range(1, CW):
                value = jnp.where(wants[zz] == c, found[c], value)
            out_ref[zz, :, j * LANES : (j + 1) * LANES] = value


def on_device(w_tiles, w_cols, t_tiles, t_cols, z_cols):
    t = t_tiles.reshape(SHARD, LANES)
    ids = t_cols.reshape(1, KC)
    vmem = pl.BlockSpec(memory_space=pltpu.VMEM)
    dma = pltpu.SemaphoreType.DMA
    rows = pl.pallas_call(
        main_kernel,
        out_shape=jax.ShapeDtypeStruct((3, PAIRS * CH, LANES), F32),
        in_specs=[vmem, vmem, vmem, pl.BlockSpec(memory_space=pltpu.SMEM)],
        out_specs=pl.BlockSpec(memory_space=pl.ANY),
        scratch_shapes=[
            pltpu.VMEM((SHARD, LANES), F32),
            pltpu.VMEM((PAIRS, SHARD, LANES), F32),
            pltpu.VMEM((8, LANES), jnp.int32),
            pltpu.VMEM((PAIRS, 8, LANES), jnp.int32),
            pltpu.VMEM((COLS, LANES), jnp.int32),
            pltpu.SMEM((COLS, LANES), jnp.int32),
            pltpu.VMEM((RT, WS * 64, LANES), F32),
            pltpu.VMEM((KC // 2, ROWS, LANES), F32),
            pltpu.VMEM((2 * ROWS, KDIM), BF16),
            pltpu.VMEM((PAIRS + 1, 4, SHARD, LANES), BF16),
            pltpu.VMEM((KDIM, PL * LANES), BF16),
            pltpu.VMEM((KDIM, PL * LANES), BF16),
            pltpu.VMEM((NB, PL, ROWS, LANES), F32),
            pltpu.VMEM((NB, PL, HALF, LANES), F32),
            pltpu.VMEM((NB, STEPS_A, PL, CH, LANES), F32),
            pltpu.VMEM((NB, STEPS_B, PL, CH, LANES), F32),
            pltpu.VMEM((NB, PL, CH, LANES), F32),
            dma((40,)),
            dma((40,)),
            dma,
            dma,
            dma((PAIRS,)),
            dma((PAIRS,)),
            dma((NB, len(PARTS))),
            dma((NB, len(PARTS))),
            dma((NB, 2, STEPS_A)),
            dma((NB, 2, STEPS_A)),
            dma((NB, 2, STEPS_B)),
            dma((NB, 2, STEPS_B)),
            dma((NB, 2)),
            dma((PAIRS,)),
            dma,
        ],
        compiler_params=pltpu.CompilerParams(
            collective_id=0, has_side_effects=True, vmem_limit_bytes=66 * 1000 * 1000
        ),
        name="cycle",
    )(t, ids, w_tiles, w_cols)
    picked = pl.pallas_call(
        pick_kernel,
        out_shape=jax.ShapeDtypeStruct((CW, PAIRS * RT, 8 * S), F32),
        in_specs=[vmem, vmem],
        out_specs=vmem,
        name="pick",
    )(rows, z_cols.transpose(2, 0, 1))
    return picked.transpose(1, 0, 2)[None]


def solution(mesh):
    in_specs = (
        P("pair", "col", None),
        P("pair", "col"),
        P("col", "pair", None),
        P("col", "pair"),
        P("pair", None, None),
    )
    out_specs = P("pair", None, None, "col")
    return jax.shard_map(
        on_device, mesh=mesh, in_specs=in_specs, out_specs=out_specs, check_vma=False
    )
```

```python
import functools

import jax
import jax.numpy as jnp
from jax import lax
from jax.experimental import pallas as pl
from jax.experimental.pallas import tpu as pltpu
from jax.sharding import PartitionSpec as P

MESH = pl.DeviceIdType.MESH

S = 64
LANES = 128
SIDE = 4
PAIRS = 16
NZ = 8
RT = 5
KC = 20
WS = 8
CW = 5
NB = 4
PL = 10
NH = 5
WIDE = 2
ROWS = 640
HALF = ROWS // 2
CH = 40
KDIM = KC * S
SHARD = KC * 32
COLS = 80
HS = SHARD // 2
QS = HS // 2
STEPS_A = 4
STEPS_B = 3
LATE = (16, 12, 8, 4)
DEPTH = 4
FIRST = (0, 2, 5, 7)
F32 = jnp.float32
BF16 = jnp.bfloat16
PLACES = ((0, 1), (2, 3), (4, 9), (5, 6), (7, 8))


def mix(a, b, left):
    straight = jnp.where(left, a, b)
    crossed = pltpu.roll(jnp.where(left, b, a), S, 1)
    return jnp.where(left, straight, crossed), jnp.where(left, crossed, straight)


def split(x):
    high = x.astype(BF16)
    return high, (x - high.astype(F32)).astype(BF16)


def main_kernel(
    t_ref,
    ids_ref,
    w_ref,
    w_cols_ref,
    out_ref,
    shard,
    tiles,
    ids_own,
    ids,
    inv_vec,
    inv,
    w_rows,
    w_wide,
    w_pair,
    halves,
    t_high,
    t_low,
    part,
    swap,
    acc_a,
    acc_b,
    total,
    g_send,
    g_recv,
    own_sem,
    inv_sem,
    i_send,
    i_recv,
    s_send,
    s_recv,
    a_send,
    a_recv,
    b_send,
    b_recv,
    x_send,
    x_recv,
    home_sem,
):
    p = lax.axis_index("pair")
    q = lax.axis_index("col")
    px, py = p // SIDE, lax.rem(p, SIDE)
    z, core = q // 2, lax.rem(q, 2)
    left = lax.broadcasted_iota(jnp.int32, (1, LANES), 1) < S

    def near(axis, sign):
        if axis == 0:
            there = lax.rem(px + sign + SIDE, SIDE) * SIDE + py
        else:
            there = px * SIDE + lax.rem(py + sign + SIDE, SIDE)
        return {"pair": there, "col": q}

    def along_z(step):
        return {"pair": p, "col": lax.rem(z + step + 2 * NZ, NZ) * 2 + core}

    mate = {"pair": p, "col": z * 2 + 1 - core}

    barrier = pltpu.get_barrier_semaphore()
    for d in range(1, PAIRS):
        pl.semaphore_signal(
            barrier, inc=1, device_id={"pair": lax.rem(p + d, PAIRS), "col": q}, device_id_type=MESH
        )
    for who in (mate, along_z(1), along_z(-1)):
        pl.semaphore_signal(barrier, inc=1, device_id=who, device_id_type=MESH)

    ids_own[...] = jnp.zeros_like(ids_own)
    ids_own[0:1, 0:KC] = ids_ref[...]

    for k in range(KC):
        top = t_ref[k * 32 : k * 32 + 16]
        bottom = t_ref[k * 32 + 16 : k * 32 + 32]
        for h, rows in enumerate(mix(top, bottom, left)):
            shard[pl.ds(k * 32 + h, 16, stride=2), :] = rows

    pl.semaphore_wait(barrier, PAIRS + 2)
    own_copy = pltpu.make_async_copy(shard, tiles.at[p], own_sem)
    own_copy.start()

    def slot(half, da, db):
        dx, dy = (da, db) if half == 0 else (db, da)
        return lax.rem(px + dx + SIDE, SIDE) * SIDE + lax.rem(py + dy + SIDE, SIDE)

    def hop(number, half, da, db, first, count, axis, sign):
        place = slot(half, da, db)
        rows = pl.ds(first, count)
        source = shard.at[rows] if (da, db) == (0, 0) else tiles.at[place, rows]
        return pltpu.make_async_remote_copy(
            src_ref=source,
            dst_ref=tiles.at[place, rows],
            send_sem=g_send.at[number],
            recv_sem=g_recv.at[number],
            device_id=near(axis, sign),
            device_id_type=MESH,
        )

    def landing(number, half, da, db, first, count, axis, sign):
        return pltpu.make_async_remote_copy(
            src_ref=tiles.at[slot(half, da, db), pl.ds(first, count)],
            dst_ref=tiles.at[slot(half, da, db), pl.ds(first, count)],
            send_sem=g_send.at[number],
            recv_sem=g_recv.at[number],
            device_id=near(axis, sign),
            device_id_type=MESH,
        )

    sends = []
    numbers = {}

    def go(half, kind, da, sign):
        axis_a, axis_b = (0, 1) if half == 0 else (1, 0)
        base = half * HS
        quarter = base if sign == 1 else base + QS
        if kind == "a0":
            args = (0, 0, base, HS, axis_a)
            seen = (-sign, 0)
        elif kind == "a1":
            args = (-sign, 0, quarter, QS, axis_a)
            seen = (2, 0)
        elif kind == "b0":
            args = (da, 0, base, HS, axis_b)
            seen = (da, -sign)
        else:
            args = (da, -sign, quarter, QS, axis_b)
            seen = (da, 2)
        number = len(numbers)
        numbers[half, kind, da, sign] = (number, half, *seen, *args[2:], sign)
        copy = hop(number, half, *args, sign)
        copy.start()
        sends.append(copy)

    def got(half, kind, da, sign):
        landing(*numbers[half, kind, da, sign]).wait_recv()

    both = (1, -1)
    for sign in both:
        for half in range(2):
            go(half, "a0", 0, sign)
            go(half, "b0", 0, sign)

    def send_ids(d):
        there = lax.rem(p + d, PAIRS)
        return pltpu.make_async_remote_copy(
            src_ref=ids_own,
            dst_ref=ids.at[p],
            send_sem=i_send.at[there],
            recv_sem=i_recv.at[p],
            device_id={"pair": there, "col": q},
            device_id_type=MESH,
        )

    def get_ids(d):
        source = lax.rem(p + d, PAIRS)
        return pltpu.make_async_remote_copy(
            src_ref=ids_own,
            dst_ref=ids.at[source],
            send_sem=i_send.at[source],
            recv_sem=i_recv.at[source],
            device_id={"pair": source, "col": q},
            device_id_type=MESH,
        )

    for d in range(1, PAIRS):
        send_ids(d).start()
    ids[p] = ids_own[...]

    @pl.loop(0, 64)
    def _(m):
        lanes = pl.ds(pl.multiple_of(m * LANES, LANES), LANES)
        for r in range(RT):
            w_rows[r, pl.ds(m, WS, stride=64), :] = w_ref[r, :, lanes]

    def w_dense(w):
        for r in range(RT):
            picks = [jnp.zeros((64, LANES), F32)] * 2
            for n in range(WS):
                rows = w_rows[r, n * 64 : (n + 1) * 64, :]
                for k in range(2):
                    there = jnp.where(w_cols_ref[r, n] == 2 * w + k, 1.0, 0.0)
                    picks[k] = picks[k] + there * rows
            for odd, rows in enumerate(mix(*picks, left)):
                for zz in range(NZ):
                    for c in range(2):
                        to = c * HALF + zz * CH + r * 8 + odd * 4
                        w_wide[w, to : to + 4, :] = rows[zz * 8 + c * 4 : zz * 8 + c * 4 + 4]

    def w_split(w):
        high, low = split(w_wide[w])
        w_pair[0:ROWS, w * LANES : (w + 1) * LANES] = high
        w_pair[ROWS : 2 * ROWS, w * LANES : (w + 1) * LANES] = low

    def halve(half, da, db):
        place = slot(half, da, db)

        @pl.loop(half * 4, half * 4 + 4, unroll=4)
        def _(n):
            rows = pl.ds(pl.multiple_of(n * 80, 80), 80)
            x = tiles[place, rows, :]
            for h, wide in enumerate((x, pltpu.roll(x, S, 1))):
                high, low = split(wide)
                halves[place, 2 * h, rows, :] = high
                halves[place, 2 * h + 1, rows, :] = low

    for sign in both:
        for half in range(2):
            got(half, "a0", 0, sign)
            go(half, "a1", 0, sign)
            go(half, "b0", -sign, 1)
            go(half, "b0", -sign, -1)
    own_copy.wait()
    for half in range(2):
        halve(half, 0, 0)
        halve(half, -1, 0)
        halve(half, 1, 0)

    @pl.loop(0, KC // 4)
    def _(w):
        w_dense(w)

    for sign in both:
        for half in range(2):
            got(half, "b0", 0, sign)
            go(half, "b1", 0, sign)
    for half in range(2):
        for sign in both:
            got(half, "a1", 0, sign)
        for sign in both:
            go(half, "b0", 2, sign)
    for half in range(2):
        halve(half, 0, -1)
        halve(half, 0, 1)
        halve(half, 2, 0)

    @pl.loop(KC // 4, KC // 2)
    def _(w):
        w_dense(w)

    for da in (-1, 1):
        for sign in both:
            for half in range(2):
                got(half, "b0", da, sign)
                go(half, "b1", da, sign)
        for sign in both:
            for half in range(2):
                halve(half, da, -sign)
    halves[PAIRS] = jnp.zeros((4, SHARD, LANES), BF16)
    for w in range(KC // 2):
        w_split(w)
    for sign in both:
        for half in range(2):
            got(half, "b0", 2, sign)
            go(half, "b1", 2, sign)

    for d in range(1, PAIRS):
        get_ids(d).wait_recv()
    tile_at = lax.broadcasted_iota(jnp.int32, (COLS, LANES), 0)
    found = jnp.full((COLS, LANES), PAIRS, jnp.int32)
    for n in range(PAIRS):
        found = jnp.where(ids[n, 0:1, :] == tile_at, n, found)
    inv_vec[...] = found
    table = pltpu.make_async_copy(inv_vec, inv, inv_sem)
    table.start()
    table.wait()
    for sign in both:
        for half in range(2):
            halve(half, 2, -sign)
    for da in (0, -1, 1, 2):
        for half in range(2):
            for sign in both:
                got(half, "b1", da, sign)
            halve(half, da, 2)

    def planes_of(h):
        return pl.ds(WIDE * h, WIDE)

    def pair_swap(b, h):
        return pltpu.make_async_remote_copy(
            src_ref=part.at[b, planes_of(h), pl.ds((1 - core) * HALF, HALF)],
            dst_ref=swap.at[b, planes_of(h)],
            send_sem=s_send.at[b, h],
            recv_sem=s_recv.at[b, h],
            device_id=mate,
            device_id_type=MESH,
        )

    def way(b, h):
        return 1 - 2 * lax.rem(b + h, 2)

    def own_rows(step):
        return pl.ds(core * HALF + lax.rem(z + step + 2 * NZ, NZ) * CH, CH)

    def chain(b, h, k, length, acc, send, recv, sign):
        planes = planes_of(h)
        source = part.at[b, planes, own_rows(length * sign)] if k == 0 else acc.at[b, k - 1, planes]
        return pltpu.make_async_remote_copy(
            src_ref=source,
            dst_ref=acc.at[b, k, planes],
            send_sem=send.at[b, h, k],
            recv_sem=recv.at[b, h, k],
            device_id=along_z(sign),
            device_id_type=MESH,
        )

    def chain_a(b, h, k):
        return chain(b, h, k, STEPS_A, acc_a, a_send, a_recv, way(b, h))

    def chain_b(b, h, k):
        return chain(b, h, k, STEPS_B, acc_b, b_send, b_recv, -way(b, h))

    def group_pair(b, i):
        return lax.rem(2 * b + i + 1 + p // 2, PAIRS // 2)

    def outward(b, g):
        there = group_pair(b, g // 2) * 2 + g % 2
        return there, pltpu.make_async_remote_copy(
            src_ref=total.at[b, pl.ds(FIRST[g], 3)],
            dst_ref=out_ref.at[:, pl.ds(p * CH, CH)],
            send_sem=x_send.at[b, g],
            recv_sem=x_recv.at[p],
            device_id={"pair": there, "col": q},
            device_id_type=MESH,
        )

    def homeward(b, g):
        return pltpu.make_async_copy(
            total.at[b, pl.ds(FIRST[g], 3)], out_ref.at[:, pl.ds(p * CH, CH)], home_sem
        )

    def begin(b, h):
        pair_swap(b, h).wait_recv()
        part[b, planes_of(h), pl.ds(core * HALF, HALF), :] += swap[b, planes_of(h)]
        chain_a(b, h, 0).start()
        chain_b(b, h, 0).start()

    def onward(k):
        def act(b, h):
            sign = way(b, h)
            planes = planes_of(h)
            chain_a(b, h, k).wait_recv()
            acc_a[b, k, planes] += part[b, planes, own_rows((STEPS_A - 1 - k) * sign), :]
            chain_a(b, h, k + 1).start()
            chain_b(b, h, k).wait_recv()
            if k < STEPS_B - 1:
                acc_b[b, k, planes] += part[b, planes, own_rows(-(STEPS_B - 1 - k) * sign), :]
                chain_b(b, h, k + 1).start()

        return act

    def finish(b, h):
        planes = planes_of(h)
        chain_a(b, h, 3).wait_recv()
        total[b, planes] = part[b, planes, own_rows(0), :] + acc_a[b, 3, planes] + acc_b[b, 2, planes]
        if h > 0:
            there, copy = outward(b, h - 1)

            @pl.when(there != p)
            def _():
                copy.start()

            @pl.when(there == p)
            def _():
                homeward(b, h - 1).start()

    def expand(b, h):
        base = [group_pair(b, i) * 2 * CW for i in range(2)]

        @pl.loop(0, KC, unroll=5)
        def _(k):
            rows = pl.ds(pl.multiple_of(k * 32, 32), 32)
            for i in range(WIDE):
                pair, plane = divmod(WIDE * h + i, len(PLACES))
                one, two = PLACES[plane]
                a = inv[base[pair] + one, k]
                c = inv[base[pair] + two, k]
                for g in range(2):
                    to = pl.ds(pl.multiple_of(k * S + g * 32, 32), 32)
                    for n, wide in enumerate((t_high, t_low)):
                        wide[to, i * LANES : (i + 1) * LANES] = jnp.where(
                            left,
                            halves[a, 2 * g + n, rows, :],
                            halves[c, 2 - 2 * g + n, rows, :],
                        )

    def multiply(b, h):
        wide = jnp.dot(w_pair[...], t_high[...], preferred_element_type=F32)
        thin = jnp.dot(w_pair[0:ROWS, :], t_low[...], preferred_element_type=F32)
        sums = wide[0:ROWS] + (wide[ROWS:] + thin)
        for i in range(WIDE):
            part[b, WIDE * h + i] = sums[:, i * LANES : (i + 1) * LANES]
        pair_swap(b, h).start()

    @pl.loop(0, NB + DEPTH)
    def _(t):
        for h in range(NH):

            def only(late, act):
                b, part_of = t + (h - late) // NH, (h - late) % NH

                @pl.when(jnp.logical_and(b >= 0, b < NB))
                def _():
                    act(b, part_of)

            only(LATE[0], finish)
            only(LATE[1], onward(2))
            only(LATE[2], onward(1))
            only(LATE[3], onward(0))
            only(0, expand)
            only(0, multiply)
            only(1, begin)

    for d in range(1, PAIRS):
        source = lax.rem(p + d, PAIRS)
        pltpu.make_async_remote_copy(
            src_ref=total.at[0, pl.ds(0, 3)],
            dst_ref=out_ref.at[:, pl.ds(source * CH, CH)],
            send_sem=x_send.at[0, 0],
            recv_sem=x_recv.at[source],
            device_id={"pair": source, "col": q},
            device_id_type=MESH,
        ).wait_recv()

    @pl.loop(0, NB)
    def _(b):
        for h in range(NH):
            pair_swap(b, h).wait_send()
            for k in range(STEPS_A):
                chain_a(b, h, k).wait_send()
            for k in range(STEPS_B):
                chain_b(b, h, k).wait_send()
        for g in range(len(FIRST)):
            there, copy = outward(b, g)

            @pl.when(there != p)
            def _():
                copy.wait_send()

            @pl.when(there == p)
            def _():
                homeward(b, g).wait()

    for copy in sends:
        copy.wait_send()
    for d in range(1, PAIRS):
        send_ids(d).wait_send()


def pick_kernel(rows_ref, z_cols_ref, out_ref):
    odd = lax.rem(lax.axis_index("pair"), 2)
    left = lax.broadcasted_iota(jnp.int32, (1, LANES), 1) < S
    planes = (
        jnp.where(odd == 1, 1, 0),
        jnp.where(odd == 1, 2, 1),
        jnp.where(odd == 1, 0, 2),
    )
    count = out_ref.shape[1]
    across = lax.broadcasted_iota(jnp.int32, (count, count), 1)
    diagonal = lax.broadcasted_iota(jnp.int32, (count, count), 0) == across
    wants = []
    for zz in range(CW):
        row = z_cols_ref[zz].astype(F32)
        want = jnp.sum(jnp.where(diagonal, row, 0.0), axis=1, keepdims=True)
        wants.append(jnp.broadcast_to(want, (count, LANES)))
    for j in range(4):
        found = []
        for n, plane in enumerate(planes):
            one = rows_ref[plane, pl.ds(j, count, stride=8), :]
            two = rows_ref[plane, pl.ds(4 + j, count, stride=8), :]
            lefts, rights = mix(one, two, left)
            if n < 2:
                found += [lefts, rights]
            else:
                found.append(jnp.where(odd == 1, rights, lefts))
        for zz in range(CW):
            value = found[0]
            for c in range(1, CW):
                value = jnp.where(wants[zz] == c, found[c], value)
            out_ref[zz, :, j * LANES : (j + 1) * LANES] = value


def on_device(w_tiles, w_cols, t_tiles, t_cols, z_cols):
    t = t_tiles.reshape(SHARD, LANES)
    ids = t_cols.reshape(1, KC)
    vmem = pl.BlockSpec(memory_space=pltpu.VMEM)
    dma = pltpu.SemaphoreType.DMA
    rows = pl.pallas_call(
        main_kernel,
        out_shape=jax.ShapeDtypeStruct((3, PAIRS * CH, LANES), F32),
        in_specs=[vmem, vmem, vmem, pl.BlockSpec(memory_space=pltpu.SMEM)],
        out_specs=pl.BlockSpec(memory_space=pl.ANY),
        scratch_shapes=[
            pltpu.VMEM((SHARD, LANES), F32),
            pltpu.VMEM((PAIRS, SHARD, LANES), F32),
            pltpu.VMEM((8, LANES), jnp.int32),
            pltpu.VMEM((PAIRS, 8, LANES), jnp.int32),
            pltpu.VMEM((COLS, LANES), jnp.int32),
            pltpu.SMEM((COLS, LANES), jnp.int32),
            pltpu.VMEM((RT, WS * 64, LANES), F32),
            pltpu.VMEM((KC // 2, ROWS, LANES), F32),
            pltpu.VMEM((2 * ROWS, KDIM), BF16),
            pltpu.VMEM((PAIRS + 1, 4, SHARD, LANES), BF16),
            pltpu.VMEM((KDIM, WIDE * LANES), BF16),
            pltpu.VMEM((KDIM, WIDE * LANES), BF16),
            pltpu.VMEM((NB, PL, ROWS, LANES), F32),
            pltpu.VMEM((NB, PL, HALF, LANES), F32),
            pltpu.VMEM((NB, STEPS_A, PL, CH, LANES), F32),
            pltpu.VMEM((NB, STEPS_B, PL, CH, LANES), F32),
            pltpu.VMEM((NB, PL, CH, LANES), F32),
            dma((40,)),
            dma((40,)),
            dma,
            dma,
            dma((PAIRS,)),
            dma((PAIRS,)),
            dma((NB, NH)),
            dma((NB, NH)),
            dma((NB, NH, STEPS_A)),
            dma((NB, NH, STEPS_A)),
            dma((NB, NH, STEPS_B)),
            dma((NB, NH, STEPS_B)),
            dma((NB, len(FIRST))),
            dma((PAIRS,)),
            dma,
        ],
        compiler_params=pltpu.CompilerParams(
            collective_id=0, has_side_effects=True, vmem_limit_bytes=66 * 1000 * 1000
        ),
        name="cycle",
    )(t, ids, w_tiles, w_cols)
    picked = pl.pallas_call(
        pick_kernel,
        out_shape=jax.ShapeDtypeStruct((CW, PAIRS * RT, 8 * S), F32),
        in_specs=[vmem, vmem],
        out_specs=vmem,
        name="pick",
    )(rows, z_cols.transpose(2, 0, 1))
    return picked.transpose(1, 0, 2)[None]


def solution(mesh):
    in_specs = (
        P("pair", "col", None),
        P("pair", "col"),
        P("col", "pair", None),
        P("col", "pair"),
        P("pair", None, None),
    )
    out_specs = P("pair", None, None, "col")
    return jax.shard_map(
        on_device, mesh=mesh, in_specs=in_specs, out_specs=out_specs, check_vma=False
    )
```

```python
import functools

import jax
import jax.numpy as jnp
from jax import lax
from jax.experimental import pallas as pl
from jax.experimental.pallas import tpu as pltpu
from jax.sharding import PartitionSpec as P

MESH = pl.DeviceIdType.MESH

S = 64
LANES = 128
SIDE = 4
PAIRS = 16
NZ = 8
RT = 5
KC = 20
WS = 8
CW = 5
NB = 4
PL = 10
NH = 5
WIDE = 2
ROWS = 640
HALF = ROWS // 2
CH = 40
KDIM = KC * S
SHARD = KC * 32
COLS = 80
HS = SHARD // 2
QS = HS // 2
STEPS_A = 4
STEPS_B = 3
LATE = (16, 12, 8, 4)
DEPTH = 4
FIRST = (0, 2, 5, 7)
F32 = jnp.float32
BF16 = jnp.bfloat16
PLACES = ((0, 1), (2, 3), (4, 9), (5, 6), (7, 8))


def mix(a, b, left):
    straight = jnp.where(left, a, b)
    crossed = pltpu.roll(jnp.where(left, b, a), S, 1)
    return jnp.where(left, straight, crossed), jnp.where(left, crossed, straight)


def split(x):
    high = x.astype(BF16)
    return high, (x - high.astype(F32)).astype(BF16)


def main_kernel(
    t_ref,
    ids_ref,
    w_ref,
    w_cols_ref,
    out_ref,
    shard,
    tiles,
    ids_own,
    ids,
    inv_vec,
    inv,
    w_rows,
    w_wide,
    w_pair,
    halves,
    t_high,
    t_low,
    part,
    swap,
    acc_a,
    acc_b,
    total,
    g_send,
    g_recv,
    own_sem,
    inv_sem,
    i_send,
    i_recv,
    s_send,
    s_recv,
    a_send,
    a_recv,
    b_send,
    b_recv,
    x_send,
    x_recv,
    home_sem,
):
    p = lax.axis_index("pair")
    q = lax.axis_index("col")
    px, py = p // SIDE, lax.rem(p, SIDE)
    z, core = q // 2, lax.rem(q, 2)
    left = lax.broadcasted_iota(jnp.int32, (1, LANES), 1) < S

    def near(axis, sign):
        if axis == 0:
            there = lax.rem(px + sign + SIDE, SIDE) * SIDE + py
        else:
            there = px * SIDE + lax.rem(py + sign + SIDE, SIDE)
        return {"pair": there, "col": q}

    def along_z(step):
        return {"pair": p, "col": lax.rem(z + step + 2 * NZ, NZ) * 2 + core}

    mate = {"pair": p, "col": z * 2 + 1 - core}

    barrier = pltpu.get_barrier_semaphore()
    for d in range(1, PAIRS):
        pl.semaphore_signal(
            barrier, inc=1, device_id={"pair": lax.rem(p + d, PAIRS), "col": q}, device_id_type=MESH
        )
    for who in (mate, along_z(1), along_z(-1)):
        pl.semaphore_signal(barrier, inc=1, device_id=who, device_id_type=MESH)

    ids_own[...] = jnp.zeros_like(ids_own)
    ids_own[0:1, 0:KC] = ids_ref[...]

    for k in range(KC):
        top = t_ref[k * 32 : k * 32 + 16]
        bottom = t_ref[k * 32 + 16 : k * 32 + 32]
        for h, rows in enumerate(mix(top, bottom, left)):
            shard[pl.ds(k * 32 + h, 16, stride=2), :] = rows

    pl.semaphore_wait(barrier, PAIRS + 2)
    own_copy = pltpu.make_async_copy(shard, tiles.at[p], own_sem)
    own_copy.start()

    def slot(half, da, db):
        dx, dy = (da, db) if half == 0 else (db, da)
        return lax.rem(px + dx + SIDE, SIDE) * SIDE + lax.rem(py + dy + SIDE, SIDE)

    def hop(number, half, da, db, first, count, axis, sign):
        place = slot(half, da, db)
        rows = pl.ds(first, count)
        source = shard.at[rows] if (da, db) == (0, 0) else tiles.at[place, rows]
        return pltpu.make_async_remote_copy(
            src_ref=source,
            dst_ref=tiles.at[place, rows],
            send_sem=g_send.at[number],
            recv_sem=g_recv.at[number],
            device_id=near(axis, sign),
            device_id_type=MESH,
        )

    def landing(number, half, da, db, first, count, axis, sign):
        return pltpu.make_async_remote_copy(
            src_ref=tiles.at[slot(half, da, db), pl.ds(first, count)],
            dst_ref=tiles.at[slot(half, da, db), pl.ds(first, count)],
            send_sem=g_send.at[number],
            recv_sem=g_recv.at[number],
            device_id=near(axis, sign),
            device_id_type=MESH,
        )

    sends = []
    numbers = {}

    def go(half, kind, da, sign):
        axis_a, axis_b = (0, 1) if half == 0 else (1, 0)
        base = half * HS
        quarter = base if sign == 1 else base + QS
        if kind == "a0":
            args = (0, 0, base, HS, axis_a)
            seen = (-sign, 0)
        elif kind == "a1":
            args = (-sign, 0, quarter, QS, axis_a)
            seen = (2, 0)
        elif kind == "b0":
            args = (da, 0, base, HS, axis_b)
            seen = (da, -sign)
        else:
            args = (da, -sign, quarter, QS, axis_b)
            seen = (da, 2)
        number = len(numbers)
        numbers[half, kind, da, sign] = (number, half, *seen, *args[2:], sign)
        copy = hop(number, half, *args, sign)
        copy.start()
        sends.append(copy)

    def got(half, kind, da, sign):
        landing(*numbers[half, kind, da, sign]).wait_recv()

    both = (1, -1)
    for sign in both:
        for half in range(2):
            go(half, "a0", 0, sign)
            go(half, "b0", 0, sign)

    def send_ids(d):
        there = lax.rem(p + d, PAIRS)
        return pltpu.make_async_remote_copy(
            src_ref=ids_own,
            dst_ref=ids.at[p],
            send_sem=i_send.at[there],
            recv_sem=i_recv.at[p],
            device_id={"pair": there, "col": q},
            device_id_type=MESH,
        )

    def get_ids(d):
        source = lax.rem(p + d, PAIRS)
        return pltpu.make_async_remote_copy(
            src_ref=ids_own,
            dst_ref=ids.at[source],
            send_sem=i_send.at[source],
            recv_sem=i_recv.at[source],
            device_id={"pair": source, "col": q},
            device_id_type=MESH,
        )

    for d in range(1, PAIRS):
        send_ids(d).start()
    ids[p] = ids_own[...]

    @pl.loop(0, 64)
    def _(m):
        lanes = pl.ds(pl.multiple_of(m * LANES, LANES), LANES)
        for r in range(RT):
            w_rows[r, pl.ds(m, WS, stride=64), :] = w_ref[r, :, lanes]

    def w_dense(w):
        for r in range(RT):
            picks = [jnp.zeros((64, LANES), F32)] * 2
            for n in range(WS):
                rows = w_rows[r, n * 64 : (n + 1) * 64, :]
                for k in range(2):
                    there = jnp.where(w_cols_ref[r, n] == 2 * w + k, 1.0, 0.0)
                    picks[k] = picks[k] + there * rows
            for odd, rows in enumerate(mix(*picks, left)):
                for zz in range(NZ):
                    for c in range(2):
                        to = c * HALF + zz * CH + r * 8 + odd * 4
                        w_wide[w, to : to + 4, :] = rows[zz * 8 + c * 4 : zz * 8 + c * 4 + 4]

    def w_split(w):
        high, low = split(w_wide[w])
        w_pair[0:ROWS, w * LANES : (w + 1) * LANES] = high
        w_pair[ROWS : 2 * ROWS, w * LANES : (w + 1) * LANES] = low

    def halve(half, da, db):
        place = slot(half, da, db)

        @pl.loop(half * 2, half * 2 + 2, unroll=2)
        def _(n):
            rows = pl.ds(pl.multiple_of(n * 160, 160), 160)
            x = tiles[place, rows, :]
            for h, wide in enumerate((x, pltpu.roll(x, S, 1))):
                high, low = split(wide)
                halves[place, 2 * h, rows, :] = high
                halves[place, 2 * h + 1, rows, :] = low

    for sign in both:
        for half in range(2):
            got(half, "a0", 0, sign)
            go(half, "a1", 0, sign)
            go(half, "b0", -sign, 1)
            go(half, "b0", -sign, -1)
    own_copy.wait()
    for half in range(2):
        halve(half, 0, 0)
        halve(half, -1, 0)
        halve(half, 1, 0)

    @pl.loop(0, KC // 4)
    def _(w):
        w_dense(w)

    for sign in both:
        for half in range(2):
            got(half, "b0", 0, sign)
            go(half, "b1", 0, sign)
    for half in range(2):
        for sign in both:
            got(half, "a1", 0, sign)
        for sign in both:
            go(half, "b0", 2, sign)
    for half in range(2):
        halve(half, 0, -1)
        halve(half, 0, 1)
        halve(half, 2, 0)

    @pl.loop(KC // 4, KC // 2)
    def _(w):
        w_dense(w)

    for da in (-1, 1):
        for sign in both:
            for half in range(2):
                got(half, "b0", da, sign)
                go(half, "b1", da, sign)
        for sign in both:
            for half in range(2):
                halve(half, da, -sign)
    for d in range(1, PAIRS):
        get_ids(d).wait_recv()
    tile_at = lax.broadcasted_iota(jnp.int32, (COLS, LANES), 0)
    found = jnp.full((COLS, LANES), PAIRS, jnp.int32)
    for n in range(PAIRS):
        found = jnp.where(ids[n, 0:1, :] == tile_at, n, found)
    inv_vec[...] = found
    table = pltpu.make_async_copy(inv_vec, inv, inv_sem)
    table.start()
    halves[PAIRS] = jnp.zeros((4, SHARD, LANES), BF16)
    for w in range(KC // 2):
        w_split(w)
    table.wait()
    for sign in both:
        for half in range(2):
            got(half, "b0", 2, sign)
            go(half, "b1", 2, sign)

    for sign in both:
        for half in range(2):
            halve(half, 2, -sign)
    for da in (0, -1, 1, 2):
        for half in range(2):
            for sign in both:
                got(half, "b1", da, sign)
            halve(half, da, 2)

    def planes_of(h):
        return pl.ds(WIDE * h, WIDE)

    def pair_swap(b, h):
        return pltpu.make_async_remote_copy(
            src_ref=part.at[b, planes_of(h), pl.ds((1 - core) * HALF, HALF)],
            dst_ref=swap.at[b, planes_of(h)],
            send_sem=s_send.at[b, h],
            recv_sem=s_recv.at[b, h],
            device_id=mate,
            device_id_type=MESH,
        )

    def way(b, h):
        return 1 - 2 * lax.rem(b + h, 2)

    def own_rows(step):
        return pl.ds(core * HALF + lax.rem(z + step + 2 * NZ, NZ) * CH, CH)

    def chain(b, h, k, length, acc, send, recv, sign):
        planes = planes_of(h)
        source = part.at[b, planes, own_rows(length * sign)] if k == 0 else acc.at[b, k - 1, planes]
        return pltpu.make_async_remote_copy(
            src_ref=source,
            dst_ref=acc.at[b, k, planes],
            send_sem=send.at[b, h, k],
            recv_sem=recv.at[b, h, k],
            device_id=along_z(sign),
            device_id_type=MESH,
        )

    def chain_a(b, h, k):
        return chain(b, h, k, STEPS_A, acc_a, a_send, a_recv, way(b, h))

    def chain_b(b, h, k):
        return chain(b, h, k, STEPS_B, acc_b, b_send, b_recv, -way(b, h))

    def group_pair(b, i):
        return lax.rem(2 * b + i + 1 + p // 2, PAIRS // 2)

    def outward(b, g):
        there = group_pair(b, g // 2) * 2 + g % 2
        return there, pltpu.make_async_remote_copy(
            src_ref=total.at[b, pl.ds(FIRST[g], 3)],
            dst_ref=out_ref.at[:, pl.ds(p * CH, CH)],
            send_sem=x_send.at[b, g],
            recv_sem=x_recv.at[p],
            device_id={"pair": there, "col": q},
            device_id_type=MESH,
        )

    def homeward(b, g):
        return pltpu.make_async_copy(
            total.at[b, pl.ds(FIRST[g], 3)], out_ref.at[:, pl.ds(p * CH, CH)], home_sem
        )

    def begin(b, h):
        pair_swap(b, h).wait_recv()
        part[b, planes_of(h), pl.ds(core * HALF, HALF), :] += swap[b, planes_of(h)]
        chain_a(b, h, 0).start()
        chain_b(b, h, 0).start()

    def onward(k):
        def act(b, h):
            sign = way(b, h)
            planes = planes_of(h)
            chain_a(b, h, k).wait_recv()
            acc_a[b, k, planes] += part[b, planes, own_rows((STEPS_A - 1 - k) * sign), :]
            chain_a(b, h, k + 1).start()
            chain_b(b, h, k).wait_recv()
            if k < STEPS_B - 1:
                acc_b[b, k, planes] += part[b, planes, own_rows(-(STEPS_B - 1 - k) * sign), :]
                chain_b(b, h, k + 1).start()

        return act

    def finish(b, h):
        planes = planes_of(h)
        chain_a(b, h, 3).wait_recv()
        total[b, planes] = part[b, planes, own_rows(0), :] + acc_a[b, 3, planes] + acc_b[b, 2, planes]
        if h > 0:
            there, copy = outward(b, h - 1)

            @pl.when(there != p)
            def _():
                copy.start()

            @pl.when(there == p)
            def _():
                homeward(b, h - 1).start()

    def expand(b, h):
        base = [group_pair(b, i) * 2 * CW for i in range(2)]

        @pl.loop(0, KC, unroll=5)
        def _(k):
            rows = pl.ds(pl.multiple_of(k * 32, 32), 32)
            for i in range(WIDE):
                pair, plane = divmod(WIDE * h + i, len(PLACES))
                one, two = PLACES[plane]
                a = inv[base[pair] + one, k]
                c = inv[base[pair] + two, k]
                for g in range(2):
                    to = pl.ds(pl.multiple_of(k * S + g * 32, 32), 32)
                    for n, wide in enumerate((t_high, t_low)):
                        wide[to, i * LANES : (i + 1) * LANES] = jnp.where(
                            left,
                            halves[a, 2 * g + n, rows, :],
                            halves[c, 2 - 2 * g + n, rows, :],
                        )

    def multiply(b, h):
        wide = jnp.dot(w_pair[...], t_high[...], preferred_element_type=F32)
        thin = jnp.dot(w_pair[0:ROWS, :], t_low[...], preferred_element_type=F32)
        sums = wide[0:ROWS] + (wide[ROWS:] + thin)
        for i in range(WIDE):
            part[b, WIDE * h + i] = sums[:, i * LANES : (i + 1) * LANES]
        pair_swap(b, h).start()

    @pl.loop(0, NB + DEPTH)
    def _(t):
        for h in range(NH):

            def only(late, act):
                b, part_of = t + (h - late) // NH, (h - late) % NH

                @pl.when(jnp.logical_and(b >= 0, b < NB))
                def _():
                    act(b, part_of)

            only(LATE[0], finish)
            only(LATE[1], onward(2))
            only(LATE[2], onward(1))
            only(LATE[3], onward(0))
            only(0, expand)
            only(0, multiply)
            only(1, begin)

    for d in range(1, PAIRS):
        source = lax.rem(p + d, PAIRS)
        pltpu.make_async_remote_copy(
            src_ref=total.at[0, pl.ds(0, 3)],
            dst_ref=out_ref.at[:, pl.ds(source * CH, CH)],
            send_sem=x_send.at[0, 0],
            recv_sem=x_recv.at[source],
            device_id={"pair": source, "col": q},
            device_id_type=MESH,
        ).wait_recv()

    @pl.loop(0, NB)
    def _(b):
        for h in range(NH):
            pair_swap(b, h).wait_send()
            for k in range(STEPS_A):
                chain_a(b, h, k).wait_send()
            for k in range(STEPS_B):
                chain_b(b, h, k).wait_send()
        for g in range(len(FIRST)):
            there, copy = outward(b, g)

            @pl.when(there != p)
            def _():
                copy.wait_send()

            @pl.when(there == p)
            def _():
                homeward(b, g).wait()

    for copy in sends:
        copy.wait_send()
    for d in range(1, PAIRS):
        send_ids(d).wait_send()


def pick_kernel(rows_ref, z_cols_ref, out_ref):
    odd = lax.rem(lax.axis_index("pair"), 2)
    left = lax.broadcasted_iota(jnp.int32, (1, LANES), 1) < S
    planes = (
        jnp.where(odd == 1, 1, 0),
        jnp.where(odd == 1, 2, 1),
        jnp.where(odd == 1, 0, 2),
    )
    count = out_ref.shape[1]
    across = lax.broadcasted_iota(jnp.int32, (count, count), 1)
    diagonal = lax.broadcasted_iota(jnp.int32, (count, count), 0) == across
    wants = []
    for zz in range(CW):
        row = z_cols_ref[zz].astype(F32)
        want = jnp.sum(jnp.where(diagonal, row, 0.0), axis=1, keepdims=True)
        wants.append(jnp.broadcast_to(want, (count, LANES)))
    for j in range(4):
        found = []
        for n, plane in enumerate(planes):
            one = rows_ref[plane, pl.ds(j, count, stride=8), :]
            two = rows_ref[plane, pl.ds(4 + j, count, stride=8), :]
            lefts, rights = mix(one, two, left)
            if n < 2:
                found += [lefts, rights]
            else:
                found.append(jnp.where(odd == 1, rights, lefts))
        for zz in range(CW):
            value = found[0]
            for c in range(1, CW):
                value = jnp.where(wants[zz] == c, found[c], value)
            out_ref[zz, :, j * LANES : (j + 1) * LANES] = value


def on_device(w_tiles, w_cols, t_tiles, t_cols, z_cols):
    t = t_tiles.reshape(SHARD, LANES)
    ids = t_cols.reshape(1, KC)
    vmem = pl.BlockSpec(memory_space=pltpu.VMEM)
    dma = pltpu.SemaphoreType.DMA
    rows = pl.pallas_call(
        main_kernel,
        out_shape=jax.ShapeDtypeStruct((3, PAIRS * CH, LANES), F32),
        in_specs=[vmem, vmem, vmem, pl.BlockSpec(memory_space=pltpu.SMEM)],
        out_specs=pl.BlockSpec(memory_space=pl.ANY),
        scratch_shapes=[
            pltpu.VMEM((SHARD, LANES), F32),
            pltpu.VMEM((PAIRS, SHARD, LANES), F32),
            pltpu.VMEM((8, LANES), jnp.int32),
            pltpu.VMEM((PAIRS, 8, LANES), jnp.int32),
            pltpu.VMEM((COLS, LANES), jnp.int32),
            pltpu.SMEM((COLS, LANES), jnp.int32),
            pltpu.VMEM((RT, WS * 64, LANES), F32),
            pltpu.VMEM((KC // 2, ROWS, LANES), F32),
            pltpu.VMEM((2 * ROWS, KDIM), BF16),
            pltpu.VMEM((PAIRS + 1, 4, SHARD, LANES), BF16),
            pltpu.VMEM((KDIM, WIDE * LANES), BF16),
            pltpu.VMEM((KDIM, WIDE * LANES), BF16),
            pltpu.VMEM((NB, PL, ROWS, LANES), F32),
            pltpu.VMEM((NB, PL, HALF, LANES), F32),
            pltpu.VMEM((NB, STEPS_A, PL, CH, LANES), F32),
            pltpu.VMEM((NB, STEPS_B, PL, CH, LANES), F32),
            pltpu.VMEM((NB, PL, CH, LANES), F32),
            dma((40,)),
            dma((40,)),
            dma,
            dma,
            dma((PAIRS,)),
            dma((PAIRS,)),
            dma((NB, NH)),
            dma((NB, NH)),
            dma((NB, NH, STEPS_A)),
            dma((NB, NH, STEPS_A)),
            dma((NB, NH, STEPS_B)),
            dma((NB, NH, STEPS_B)),
            dma((NB, len(FIRST))),
            dma((PAIRS,)),
            dma,
        ],
        compiler_params=pltpu.CompilerParams(
            collective_id=0, has_side_effects=True, vmem_limit_bytes=66 * 1000 * 1000
        ),
        name="cycle",
    )(t, ids, w_tiles, w_cols)
    picked = pl.pallas_call(
        pick_kernel,
        out_shape=jax.ShapeDtypeStruct((CW, PAIRS * RT, 8 * S), F32),
        in_specs=[vmem, vmem],
        out_specs=vmem,
        name="pick",
    )(rows, z_cols.transpose(2, 0, 1))
    return picked.transpose(1, 0, 2)[None]


def solution(mesh):
    in_specs = (
        P("pair", "col", None),
        P("pair", "col"),
        P("col", "pair", None),
        P("col", "pair"),
        P("pair", None, None),
    )
    out_specs = P("pair", None, None, "col")
    return jax.shard_map(
        on_device, mesh=mesh, in_specs=in_specs, out_specs=out_specs, check_vma=False
    )
```
